32 devices in a mesh: group: 2 (over x), expert: 16 (over z, y, core).
Axes of the slice: x: 2, y: 2, z: 4, core: 2. Of those that a mesh axis runs over, the one named last changes fastest.
Arguments:
- rows: bfloat16 [4096, 1024], P(('group', 'expert')), parts along dimension 0, may hold values from -6 to 6
- cotangent: bfloat16 [4096, 1024], P(('group', 'expert')), parts along dimension 0, may hold values from -1.5 to 1.5
- up_proj: bfloat16 [1024, 65536], P(None, 'expert'), may hold values from -0.1875 to 0.1875
- down_proj: bfloat16 [65536, 1024], P('expert'), may hold values from -0.125 to 0.125
- mix_weight: float32 [8, 4], replicated, may hold values from 0.25 to 1
- task_counts: int32 [32, 8], P(('group', 'expert')), parts along dimension 0, may hold values from 1 to 18, 128 in all within a row
- expert_order: int32 [32, 32], P(('group', 'expert')), parts along dimension 0, may hold values from 0 to 31, each once within a row
Outputs:
- mixed: bfloat16 [4096, 1024], P(('group', 'expert')), parts along dimension 0
- row_gradient: bfloat16 [4096, 1024], P(('group', 'expert')), parts along dimension 0
- up_grad: bfloat16 [2048, 65536], P('group', 'expert'), parts along dimension 0
- down_grad: bfloat16 [65536, 2048], P('expert', 'group'), parts along dimension 1
The draws below stay inside these ranges and needn't reach their ends.
There are 2 independent parts, one for each index of `group`. The reference program is written for one: setup_inputs(seed, part) draws one part's arguments, and reference() takes and returns one part's arrays. A program takes and returns all parts, laid end to end along the dimension named above; an argument that names none is the same for every part. Nothing has to cross between parts.
Inputs may be any that keep to these rules, and one draw needn't show every extreme that they name: `task_counts`: in each block the 8 counts sum to 128, and one of them is exactly 18. Each row of expert_order names every expert once.
All inputs are finite; a program needn't handle non-finite values.
Results may differ from the reference program's by a relative error of at most 0.0085.
Values may be sent and summed in bfloat16 or wider, within the bound.
A program may use at most 128 MiB of HBM per device.

```python
import math
from functools import partial
import jax
import jax.numpy as jnp
import numpy as np
from jax import lax

D = 1024
FF = 2048
EXPERTS = 32
TASKS = 8
K = 4
TOKEN_BLOCK_ROWS = 128
CAP = 18
ROWS = 2048
N_EXPERT = 16


def steps_of(own_key, dims, cuts, smallest, top_value):
    level, own = 1.0, jax.random.fold_in(own_key, 6)
    for dim, blocks in cuts:
        draws = jnp.exp(jax.random.uniform(jax.random.fold_in(own, dim), (blocks,), jnp.float32, smallest / len(cuts), top_value / len(cuts)))
        level = level * jnp.repeat(draws, dims[dim] // blocks).reshape([-1 if axis == dim else 1 for axis in range(len(dims))])
    return level


def length_profile(amount, total, reach, skew):
    loads = [(1 << 20) // math.isqrt(rank ** skew) + 1 for rank in range(2, amount + 1)]
    spare, given = total - reach - (amount - 1), [1] * (amount - 1)
    while spare > 0:
        movable = [i for i in range(amount - 1) if given[i] < reach]
        whole, remaining = sum([loads[i] for i in movable]), spare
        for i in movable:
            more = min(reach - given[i], max(1, remaining * loads[i] // whole), spare)
            given[i] = given[i] + more
            spare = spare - more
    return np.array([reach] + given)


def uneven_parts(rng, amount, total, limit, slope):
    if amount == 2:
        one = jax.random.randint(rng, (), max(1, total - limit), min(limit, total - 1) + 1)
        return jnp.stack([one, total - one])
    sizes = jnp.asarray(length_profile(amount, total, limit, slope), jnp.int32)
    couples = (amount - 1) // 2
    source_of, receiver = sizes[1:1 + 2 * couples:2], sizes[2:2 + 2 * couples:2]
    room = jnp.minimum(source_of - 1, limit - receiver)
    shifted = jax.random.randint(jax.random.fold_in(rng, 1), (couples,), 0, 1 << 20) % (room + 1)
    sizes = sizes.at[1:1 + 2 * couples:2].set(source_of - shifted).at[2:2 + 2 * couples:2].set(receiver + shifted)
    return sizes[jax.random.permutation(jax.random.fold_in(rng, 2), amount)]


def gaussian(key, shape, width, most, split=(), kind=jnp.bfloat16):
    result = jax.random.normal(key, shape, jnp.float32) * width
    if len(split) > 0:
        result = steps_of(key, shape, split, -0.22, 0.18) * result
    return jnp.clip(result, min=-most, max=most).astype(kind)


def setup_inputs(seed: int = 0, part: int = 0) -> dict:
    streams_of = jax.random.split(jax.random.key(seed), 8)
    part_splits = jax.random.split(jax.random.fold_in(streams_of[7], part), 8)
    rows = gaussian(part_splits[0], (ROWS, D), 1.0, 6.0, ((0, 16),))
    cotangent = gaussian(part_splits[1], (ROWS, D), 0.25, 1.5, ((0, 16),))
    up_proj = gaussian(streams_of[2], (D, EXPERTS * FF), D ** -0.5, 0.1875, ((1, 16),))
    down_proj = gaussian(streams_of[3], (EXPERTS * FF, D), FF ** -0.5, 0.125, ((0, 16),))
    mix_weight = jnp.clip(jnp.exp(jax.random.uniform(streams_of[4], (TASKS, K), jnp.float32, math.log(0.25), math.log(1.0))), 0.25, 1.0)
    task_counts = jax.vmap(lambda own: uneven_parts(own, TASKS, TOKEN_BLOCK_ROWS, CAP, 2))(jax.random.split(part_splits[5], N_EXPERT)).reshape((N_EXPERT, TASKS)).astype(jnp.int32)
    expert_order = jax.vmap(lambda own: jax.random.permutation(own, EXPERTS))(jax.random.split(part_splits[6], N_EXPERT)).reshape((N_EXPERT, EXPERTS)).astype(jnp.int32)
    return {"rows": rows, "cotangent": cotangent, "up_proj": up_proj, "down_proj": down_proj, "mix_weight": mix_weight, "task_counts": task_counts, "expert_order": expert_order}


def block_route(counts, expert_list, mix_flat, row_total):
    counts = counts.astype(jnp.int32)
    firsts = (jnp.cumsum(counts) - counts).astype(jnp.int32)
    labels = jnp.arange(EXPERTS, dtype=jnp.int32)
    matches = expert_list[None, :].astype(jnp.int32) == labels[:, None]
    position = jnp.sum(jnp.where(matches, labels[None, :], 0), axis=1).astype(jnp.int32)
    task_of = position // K
    task_match = task_of[:, None] == jnp.arange(TASKS, dtype=jnp.int32)[None, :]
    count_of = jnp.sum(jnp.where(task_match, counts[None, :], 0), axis=1).astype(jnp.int32)
    first_of = jnp.sum(jnp.where(task_match, firsts[None, :], 0), axis=1).astype(jnp.int32)
    weight_of = jnp.sum(jnp.where(matches, mix_flat[None, :], jnp.zeros_like(mix_flat)[None, :]), axis=1)
    slot_index = jnp.arange(CAP, dtype=jnp.int32)
    filled = slot_index[None, :] < count_of[:, None]
    targets = first_of[:, None] + slot_index[None, :]
    row_index = jnp.arange(row_total, dtype=jnp.int32)
    selection_index = (targets[:, :, None] == row_index[None, None, :]) & filled[:, :, None]
    selection_index = selection_index.reshape(EXPERTS * CAP, row_total).astype(jnp.float32)
    slot_weight = jnp.where(filled, weight_of[:, None], jnp.zeros_like(weight_of)[:, None]).reshape(-1)
    return selection_index, slot_weight


def expert_step(operands):
    inputs, scaled, up_slice, down_slice = operands
    pre = jnp.dot(inputs, up_slice, preferred_element_type=jnp.float32)
    act = jax.nn.silu(pre).astype(jnp.bfloat16)
    outputs = jnp.dot(act, down_slice, preferred_element_type=jnp.float32)
    act_grad = jnp.dot(scaled, down_slice.T, preferred_element_type=jnp.float32)
    sigmoid = jax.nn.sigmoid(pre)
    pre_grad = (act_grad * sigmoid * (1.0 + pre * (1.0 - sigmoid))).astype(jnp.bfloat16)
    down_part = jnp.dot(act.T, scaled, preferred_element_type=jnp.float32).astype(jnp.bfloat16)
    up_part = jnp.dot(inputs.T, pre_grad, preferred_element_type=jnp.float32).astype(jnp.bfloat16)
    input_grad = jnp.dot(pre_grad, up_slice.T, preferred_element_type=jnp.float32)
    return outputs, input_grad, up_part, down_part


def reference(rows, cotangent, up_proj, down_proj, mix_weight, task_counts, expert_order):
    block_list = N_EXPERT
    hidden_width = rows.shape[1]
    route = partial(block_route, row_total=TOKEN_BLOCK_ROWS)
    selection_index, slot_weight = jax.vmap(route, in_axes=(0, 0, None))(task_counts, expert_order, mix_weight.reshape(-1))
    row_block_list = rows.reshape(block_list, TOKEN_BLOCK_ROWS, hidden_width).astype(jnp.float32)
    gradient_block_list = cotangent.reshape(block_list, TOKEN_BLOCK_ROWS, hidden_width).astype(jnp.float32)
    upper_bound = lax.Precision.HIGHEST
    slot_row_values = jnp.einsum('slt,stn->sln', selection_index, row_block_list, precision=upper_bound).astype(jnp.bfloat16)
    slot_gradient_rows = jnp.einsum('slt,stn->sln', selection_index, gradient_block_list, precision=upper_bound)
    scaled = (slot_weight[:, :, None] * slot_gradient_rows).astype(jnp.bfloat16)

    def by_expert(values):
        return values.reshape(block_list, EXPERTS, CAP, hidden_width).transpose(1, 0, 2, 3).reshape(EXPERTS, block_list * CAP, hidden_width)

    def grouped_per_block(values):
        return values.reshape(EXPERTS, block_list, CAP, hidden_width).transpose(1, 0, 2, 3).reshape(block_list, EXPERTS * CAP, hidden_width)

    up_slices = up_proj.reshape(hidden_width, EXPERTS, FF).transpose(1, 0, 2)
    down_slices = down_proj.reshape(EXPERTS, FF, hidden_width)
    outputs, input_gradient_rows, up_parts, down_parts = lax.map(expert_step, (by_expert(slot_row_values), by_expert(scaled), up_slices, down_slices))
    weighted_rows = grouped_per_block(outputs) * slot_weight[:, :, None]
    mixed = jnp.einsum('fua,ful->fal', selection_index, weighted_rows, precision=upper_bound).reshape(block_list * TOKEN_BLOCK_ROWS, hidden_width)
    row_gradient = jnp.einsum('fua,ful->fal', selection_index, grouped_per_block(input_gradient_rows), precision=upper_bound).reshape(block_list * TOKEN_BLOCK_ROWS, hidden_width)
    up_grad = up_parts.transpose(1, 0, 2).reshape(hidden_width, EXPERTS * FF)
    down_grad = down_parts.reshape(EXPERTS * FF, hidden_width)
    return mixed.astype(jnp.bfloat16), row_gradient.astype(jnp.bfloat16), up_grad, down_grad
```

```python
import jax
import jax.numpy as jnp
from jax import lax
from jax.experimental import pallas as pl
from jax.experimental.pallas import tpu as pltpu
from jax.sharding import PartitionSpec as P

FF = 2048
EXPERTS = 32
TASKS = 8
K = 4
CAP = 18
PLANE = 4
ROUTE_ROWS = 8


def block_route(counts, expert_list, mix_flat, row_total):
    firsts = jnp.cumsum(counts) - counts
    labels = jnp.arange(EXPERTS, dtype=jnp.int32)
    matches = expert_list[None, :] == labels[:, None]
    position = jnp.sum(jnp.where(matches, labels[None, :], 0), axis=1)
    task_of = position // K
    task_match = task_of[:, None] == jnp.arange(TASKS, dtype=jnp.int32)[None, :]
    count_of = jnp.sum(jnp.where(task_match, counts[None, :], 0), axis=1)
    first_of = jnp.sum(jnp.where(task_match, firsts[None, :], 0), axis=1)
    weight_of = jnp.sum(
        jnp.where(matches, mix_flat[None, :], jnp.zeros_like(mix_flat)[None, :]), axis=1
    )
    slot_index = jnp.arange(CAP, dtype=jnp.int32)
    filled = slot_index[None, :] < count_of[:, None]
    targets = first_of[:, None] + slot_index[None, :]
    row_index = jnp.arange(row_total, dtype=jnp.int32)
    selection_index = (targets[:, :, None] == row_index[None, None, :]) & filled[:, :, None]
    selection_index = selection_index.reshape(EXPERTS * CAP, row_total).astype(jnp.float32)
    slot_weight = jnp.where(filled, weight_of[:, None], jnp.zeros_like(weight_of)[:, None]).reshape(
        -1
    )
    return (selection_index, slot_weight)


def to_owners(values, copies, owners):
    if copies > 1:
        return jnp.repeat(values, copies, axis=0)
    return values.reshape((owners, -1) + values.shape[2:])


def from_owners(values, copies, hidden_width):
    if copies > 1:
        return jnp.sum(values.reshape(EXPERTS, copies, CAP, hidden_width), axis=1)
    return values.reshape(EXPERTS, CAP, hidden_width)


def forward_part(got_rows, up_local, down_local, owners, local_count, slot_count):
    hidden_width = got_rows.shape[-1]
    inputs = got_rows.reshape(owners, local_count, slot_count, hidden_width)
    pre = jnp.einsum("nlcd,dlf->nlcf", inputs, up_local, preferred_element_type=jnp.float32)
    act = jax.nn.silu(pre).astype(jnp.bfloat16)
    outputs = jnp.einsum("nlcf,lfd->nlcd", act, down_local, preferred_element_type=jnp.float32)
    return (inputs, pre, act, outputs.reshape(owners, local_count * slot_count, hidden_width))


def backward_part(
    inputs, got_grads, pre, act, up_local, down_local, owners, local_count, slot_count
):
    hidden_width = inputs.shape[-1]
    scaled = got_grads.reshape(owners, local_count, slot_count, hidden_width)
    act_grad = jnp.einsum("nlcd,lfd->nlcf", scaled, down_local, preferred_element_type=jnp.float32)
    sigmoid = jax.nn.sigmoid(pre)
    pre_grad = (act_grad * sigmoid * (1.0 + pre * (1.0 - sigmoid))).astype(jnp.bfloat16)
    down_grad = jnp.einsum("nlcf,nlcd->lfd", act, scaled, preferred_element_type=jnp.float32)
    up_grad = jnp.einsum("nlcd,nlcf->dlf", inputs, pre_grad, preferred_element_type=jnp.float32)
    partial_grads = jnp.einsum(
        "nlcf,dlf->nlcd", pre_grad, up_local, preferred_element_type=jnp.float32
    )
    units = up_local.shape[1] * up_local.shape[2]
    return (
        up_grad.reshape(hidden_width, units),
        down_grad.reshape(units, hidden_width),
        partial_grads.reshape(owners, local_count * slot_count, hidden_width),
    )


def direct_plan(rows, cotangent, up_proj, down_proj, mix_weight, task_counts, expert_order):
    owners = lax.axis_size("expert")
    row_total = rows.shape[0]
    hidden_width = rows.shape[1]
    units = up_proj.shape[1]
    local_units = min(units, FF)
    local_count = max(units // FF, 1)
    copies = max(FF // units, 1)
    selection_index, slot_weight = block_route(
        task_counts[0], expert_order[0], mix_weight.reshape(-1), row_total
    )
    select_half = selection_index.astype(jnp.bfloat16)
    slot_row_values = jnp.dot(select_half, rows, preferred_element_type=jnp.float32).astype(
        jnp.bfloat16
    )
    slot_gradient_rows = jnp.dot(select_half, cotangent, preferred_element_type=jnp.float32)
    scaled = (slot_weight[:, None] * slot_gradient_rows).astype(jnp.bfloat16)
    upper_bound = lax.Precision.HIGHEST
    sent_rows = to_owners(slot_row_values.reshape(EXPERTS, CAP, hidden_width), copies, owners)
    sent_grads = to_owners(scaled.reshape(EXPERTS, CAP, hidden_width), copies, owners)
    up_local = up_proj.reshape(hidden_width, local_count, local_units)
    down_local = down_proj.reshape(local_count, local_units, hidden_width)
    got_rows = lax.all_to_all(sent_rows, "expert", split_axis=0, concat_axis=0, tiled=True)
    inputs, pre, act, outputs = forward_part(
        got_rows, up_local, down_local, owners, local_count, CAP
    )
    back_out = lax.all_to_all(outputs, "expert", split_axis=0, concat_axis=0, tiled=True)
    got_grads = lax.all_to_all(sent_grads, "expert", split_axis=0, concat_axis=0, tiled=True)
    up_full, down_full, partial_grads = backward_part(
        inputs, got_grads, pre, act, up_local, down_local, owners, local_count, CAP
    )
    back_grads = lax.all_to_all(partial_grads, "expert", split_axis=0, concat_axis=0, tiled=True)
    up_grad = up_full.astype(jnp.bfloat16)
    down_grad = down_full.astype(jnp.bfloat16)
    returned = from_owners(back_out, copies, hidden_width).reshape(EXPERTS * CAP, hidden_width)
    summed_grads = from_owners(back_grads, copies, hidden_width).reshape(
        EXPERTS * CAP, hidden_width
    )
    weighted_rows = returned * slot_weight[:, None]
    mixed = jnp.dot(selection_index.T, weighted_rows, precision=upper_bound).astype(jnp.bfloat16)
    row_gradient = jnp.dot(selection_index.T, summed_grads, precision=upper_bound).astype(
        jnp.bfloat16
    )
    return (mixed, row_gradient, up_grad, down_grad)


def step_pairs(line, sources, shift):
    return [(z * PLANE + p, (z + shift) * PLANE + p) for z in sources for p in range(PLANE)]


def gather_line(values, line):
    up, down, ups, downs = values, values, [], []
    for k in range(1, line):
        up = lax.ppermute(up, "expert", step_pairs(line, range(k - 1, line - 1), 1))
        down = lax.ppermute(down, "expert", step_pairs(line, range(1, line - k + 1), -1))
        ups.append(up)
        downs.append(down)
    blocks = [values] + [ups[k - 1] + downs[line - k - 1] for k in range(1, line)]
    return blocks, (ups, downs)


def reduce_line(own, line):
    total = own[0]
    for shift in (1, -1):
        passed = None
        for far in range(line - 1, 0, -1):
            mine = own[line - far] if shift == 1 else own[far]
            passed = mine if passed is None else mine + passed.astype(jnp.float32)
            sources = range(0, line - far) if shift == 1 else range(far, line)
            passed = lax.ppermute(
                passed.astype(jnp.bfloat16), "expert", step_pairs(line, sources, shift)
            )
        total = total + passed.astype(jnp.float32)
    return total


def swap_plane(parts, owners):
    got = [parts[0]]
    for m in range(1, PLANE):
        pairs = [(i, i - i % PLANE + ((i % PLANE) ^ m)) for i in range(owners)]
        got.append(lax.ppermute(parts[m], "expert", pairs))
    return got


def plane_route(counts, orders, mix_flat, me, local_count, row_total):
    line = counts.shape[0]
    firsts = jnp.cumsum(counts, axis=1) - counts
    place = (me % PLANE) ^ jnp.arange(PLANE, dtype=jnp.int32)
    labels = (me - me % PLANE + place)[:, None] * local_count + jnp.arange(
        local_count, dtype=jnp.int32
    )
    matches = orders[None, None] == labels[:, :, None, None]

    def per_task(values):
        spread = jnp.repeat(values, K, axis=1)
        return jnp.sum(jnp.where(matches, spread[None, None], 0), axis=-1)

    count_of, first_of = per_task(counts), per_task(firsts)
    weight_of = jnp.sum(jnp.where(matches, mix_flat[None, None, None], 0.0), axis=-1)
    slot = jnp.arange(CAP, dtype=jnp.int32)
    filled = slot < count_of[..., None]
    base = row_total * jnp.arange(line, dtype=jnp.int32)[None, None, :, None]
    targets = jnp.where(filled, base + first_of[..., None] + slot, -1).reshape(-1)
    weights = jnp.where(filled, weight_of[..., None], 0.0).reshape(-1)
    return targets, weights


def grad_kernel(a_ref, b_ref, o_ref):
    o_ref[...] = lax.dot_general(
        a_ref[0], b_ref[0], (((0,), (0,)), ((), ())), preferred_element_type=jnp.float32
    ).astype(o_ref.dtype)


def cost(local_count, slots, units, width):
    return pl.CostEstimate(
        flops=2 * local_count * slots * units * width,
        bytes_accessed=2 * local_count * (units * width + slots * (units + width)),
        transcendentals=0,
    )


def up_grad_call(inputs, pre_grad):
    local_count, slots, width = inputs.shape
    units = pre_grad.shape[2]
    tile = min(512, units)
    return pl.pallas_call(
        grad_kernel,
        grid=(local_count, units // tile),
        in_specs=[
            pl.BlockSpec((1, slots, width), lambda l, j: (l, 0, 0)),
            pl.BlockSpec((1, slots, tile), lambda l, j: (l, 0, j)),
        ],
        out_specs=pl.BlockSpec((width, tile), lambda l, j: (0, l * (units // tile) + j)),
        out_shape=jax.ShapeDtypeStruct((width, local_count * units), jnp.bfloat16),
        cost_estimate=cost(local_count, slots, units, width),
    )(inputs, pre_grad)


def down_grad_call(act, scaled):
    local_count, slots, width = scaled.shape
    units = act.shape[2]
    tile = min(512, units)
    return pl.pallas_call(
        grad_kernel,
        grid=(local_count, units // tile),
        in_specs=[
            pl.BlockSpec((1, slots, tile), lambda l, j: (l, 0, j)),
            pl.BlockSpec((1, slots, width), lambda l, j: (l, 0, 0)),
        ],
        out_specs=pl.BlockSpec((tile, width), lambda l, j: (l * (units // tile) + j, 0)),
        out_shape=jax.ShapeDtypeStruct((local_count * units, width), jnp.bfloat16),
        cost_estimate=cost(local_count, slots, units, width),
    )(act, scaled)


def dot_nt(a, b):
    return lax.dot_general(a, b, (((1,), (1,)), ((), ())), preferred_element_type=jnp.float32)


def plane_plan(rows, cotangent, up_proj, down_proj, mix_weight, task_counts, expert_order):
    owners = lax.axis_size("expert")
    me = lax.axis_index("expert")
    line = owners // PLANE
    row_total, width = rows.shape
    local_count = up_proj.shape[1] // FF
    route = jnp.concatenate([expert_order[0], task_counts[0]]).astype(jnp.bfloat16)
    route = jnp.pad(route[None], ((0, ROUTE_ROWS - 1), (0, width - route.shape[0])))
    blocks, (ups, downs) = gather_line(jnp.concatenate([rows, route], axis=0), line)
    cotangent, ups[1], downs[1] = lax.optimization_barrier((cotangent, ups[1], downs[1]))
    cot_blocks, _ = gather_line(cotangent, line)
    routes = jnp.stack([b[row_total] for b in blocks]).astype(jnp.int32)
    targets, weights = plane_route(
        routes[:, EXPERTS : EXPERTS + TASKS],
        routes[:, :EXPERTS],
        mix_weight.reshape(-1),
        me,
        local_count,
        row_total,
    )
    select = (targets[:, None] == jnp.arange(line * row_total, dtype=jnp.int32)[None]).astype(
        jnp.bfloat16
    )
    part = local_count * line * CAP
    row_list = jnp.concatenate([b[:row_total] for b in blocks], axis=0)
    cot_list = jnp.concatenate(cot_blocks, axis=0)

    def dispatch(values, scale):
        parts = []
        for m in range(PLANE):
            own = slice(m * part, (m + 1) * part)
            picked = jnp.dot(select[own], values, preferred_element_type=jnp.float32)
            if scale is not None:
                picked = scale[own, None] * picked
            parts.append(picked.astype(jnp.bfloat16).reshape(local_count, line * CAP, width))
        return jnp.concatenate(swap_plane(parts, owners), axis=1)

    def collect(outs):
        parts = [
            outs[:, m * line * CAP : (m + 1) * line * CAP].astype(jnp.bfloat16)
            for m in range(PLANE)
        ]
        return jnp.concatenate([g.reshape(part, width) for g in swap_plane(parts, owners)], axis=0)

    def combine(slots):
        own = lax.dot_general(
            select, slots, (((0,), (0,)), ((), ())), preferred_element_type=jnp.float32
        )
        own = own.reshape(line, row_total, width)
        return reduce_line([own[k] for k in range(line)], line).astype(jnp.bfloat16)

    inputs = dispatch(row_list, None)
    scaled = dispatch(cot_list, weights)
    pres, acts, outs = [], [], []
    for l in range(local_count):
        up, down = up_proj[:, l * FF : (l + 1) * FF], down_proj[l * FF : (l + 1) * FF]
        pre = jnp.dot(inputs[l], up, preferred_element_type=jnp.float32)
        act = jax.nn.silu(pre).astype(jnp.bfloat16)
        outs.append(jnp.dot(act, down, preferred_element_type=jnp.float32).astype(jnp.bfloat16))
        pres.append(pre)
        acts.append(act)
    returned = collect(jnp.stack(outs))
    weighted = (weights[:, None] * returned.astype(jnp.float32)).astype(jnp.bfloat16)
    mixed = combine(weighted)
    pre_grads, row_grads = [], []
    for l in range(local_count):
        up, down = up_proj[:, l * FF : (l + 1) * FF], down_proj[l * FF : (l + 1) * FF]
        act_grad = dot_nt(scaled[l], down)
        sigmoid = jax.nn.sigmoid(pres[l])
        pre_grad = (act_grad * sigmoid * (1.0 + pres[l] * (1.0 - sigmoid))).astype(jnp.bfloat16)
        row_grads.append(dot_nt(pre_grad, up).astype(jnp.bfloat16))
        pre_grads.append(pre_grad)
    row_gradient = combine(collect(jnp.stack(row_grads)))
    up_grad = up_grad_call(inputs, jnp.stack(pre_grads))
    down_grad = down_grad_call(jnp.stack(acts), scaled)
    return (mixed, row_gradient, up_grad, down_grad)


def per_device(rows, cotangent, up_proj, *others):
    owners = lax.axis_size("expert")
    whole_experts = up_proj.shape[1] % FF == 0
    wide_plane = owners % PLANE == 0 and owners // PLANE >= 3
    plan = plane_plan if whole_experts and wide_plane else direct_plan
    return plan(rows, cotangent, up_proj, *others)


def solution(mesh):
    return jax.shard_map(
        per_device,
        mesh=mesh,
        in_specs=(
            P(("group", "expert"), None),
            P(("group", "expert"), None),
            P(None, "expert"),
            P("expert", None),
            P(),
            P(("group", "expert"), None),
            P(("group", "expert"), None),
        ),
        out_specs=(
            P(("group", "expert"), None),
            P(("group", "expert"), None),
            P("group", "expert"),
            P("expert", "group"),
        ),
        check_vma=False,
    )
```

```python
import functools

import jax
import jax.numpy as jnp
from jax import lax
from jax.experimental import pallas as pl
from jax.experimental.pallas import tpu as pltpu
from jax.sharding import PartitionSpec as P

FF = 2048
EXPERTS = 32
TASKS = 8
K = 4
CAP = 18
PLANE = 4
SPAN = 256
TILE = 512


def block_route(counts, expert_list, mix_flat, row_total):
    firsts = jnp.cumsum(counts) - counts
    labels = jnp.arange(EXPERTS, dtype=jnp.int32)
    matches = expert_list[None, :] == labels[:, None]
    position = jnp.sum(jnp.where(matches, labels[None, :], 0), axis=1)
    task_of = position // K
    task_match = task_of[:, None] == jnp.arange(TASKS, dtype=jnp.int32)[None, :]
    count_of = jnp.sum(jnp.where(task_match, counts[None, :], 0), axis=1)
    first_of = jnp.sum(jnp.where(task_match, firsts[None, :], 0), axis=1)
    weight_of = jnp.sum(
        jnp.where(matches, mix_flat[None, :], jnp.zeros_like(mix_flat)[None, :]), axis=1
    )
    slot_index = jnp.arange(CAP, dtype=jnp.int32)
    filled = slot_index[None, :] < count_of[:, None]
    targets = first_of[:, None] + slot_index[None, :]
    row_index = jnp.arange(row_total, dtype=jnp.int32)
    selection_index = (targets[:, :, None] == row_index[None, None, :]) & filled[:, :, None]
    selection_index = selection_index.reshape(EXPERTS * CAP, row_total).astype(jnp.float32)
    slot_weight = jnp.where(filled, weight_of[:, None], jnp.zeros_like(weight_of)[:, None]).reshape(
        -1
    )
    return (selection_index, slot_weight)


def to_owners(values, copies, owners):
    if copies > 1:
        return jnp.repeat(values, copies, axis=0)
    return values.reshape((owners, -1) + values.shape[2:])


def from_owners(values, copies, hidden_width):
    if copies > 1:
        return jnp.sum(values.reshape(EXPERTS, copies, CAP, hidden_width), axis=1)
    return values.reshape(EXPERTS, CAP, hidden_width)


def forward_part(got_rows, up_local, down_local, owners, local_count, slot_count):
    hidden_width = got_rows.shape[-1]
    inputs = got_rows.reshape(owners, local_count, slot_count, hidden_width)
    pre = jnp.einsum("nlcd,dlf->nlcf", inputs, up_local, preferred_element_type=jnp.float32)
    act = jax.nn.silu(pre).astype(jnp.bfloat16)
    outputs = jnp.einsum("nlcf,lfd->nlcd", act, down_local, preferred_element_type=jnp.float32)
    return (inputs, pre, act, outputs.reshape(owners, local_count * slot_count, hidden_width))


def backward_part(
    inputs, got_grads, pre, act, up_local, down_local, owners, local_count, slot_count
):
    hidden_width = inputs.shape[-1]
    scaled = got_grads.reshape(owners, local_count, slot_count, hidden_width)
    act_grad = jnp.einsum("nlcd,lfd->nlcf", scaled, down_local, preferred_element_type=jnp.float32)
    sigmoid = jax.nn.sigmoid(pre)
    pre_grad = (act_grad * sigmoid * (1.0 + pre * (1.0 - sigmoid))).astype(jnp.bfloat16)
    down_grad = jnp.einsum("nlcf,nlcd->lfd", act, scaled, preferred_element_type=jnp.float32)
    up_grad = jnp.einsum("nlcd,nlcf->dlf", inputs, pre_grad, preferred_element_type=jnp.float32)
    partial_grads = jnp.einsum(
        "nlcf,dlf->nlcd", pre_grad, up_local, preferred_element_type=jnp.float32
    )
    units = up_local.shape[1] * up_local.shape[2]
    return (
        up_grad.reshape(hidden_width, units),
        down_grad.reshape(units, hidden_width),
        partial_grads.reshape(owners, local_count * slot_count, hidden_width),
    )


def direct_plan(rows, cotangent, up_proj, down_proj, mix_weight, task_counts, expert_order):
    owners = lax.axis_size("expert")
    row_total = rows.shape[0]
    hidden_width = rows.shape[1]
    units = up_proj.shape[1]
    local_units = min(units, FF)
    local_count = max(units // FF, 1)
    copies = max(FF // units, 1)
    selection_index, slot_weight = block_route(
        task_counts[0], expert_order[0], mix_weight.reshape(-1), row_total
    )
    select_half = selection_index.astype(jnp.bfloat16)
    slot_row_values = jnp.dot(select_half, rows, preferred_element_type=jnp.float32).astype(
        jnp.bfloat16
    )
    slot_gradient_rows = jnp.dot(select_half, cotangent, preferred_element_type=jnp.float32)
    scaled = (slot_weight[:, None] * slot_gradient_rows).astype(jnp.bfloat16)
    upper_bound = lax.Precision.HIGHEST
    sent_rows = to_owners(slot_row_values.reshape(EXPERTS, CAP, hidden_width), copies, owners)
    sent_grads = to_owners(scaled.reshape(EXPERTS, CAP, hidden_width), copies, owners)
    up_local = up_proj.reshape(hidden_width, local_count, local_units)
    down_local = down_proj.reshape(local_count, local_units, hidden_width)
    got_rows = lax.all_to_all(sent_rows, "expert", split_axis=0, concat_axis=0, tiled=True)
    inputs, pre, act, outputs = forward_part(
        got_rows, up_local, down_local, owners, local_count, CAP
    )
    back_out = lax.all_to_all(outputs, "expert", split_axis=0, concat_axis=0, tiled=True)
    got_grads = lax.all_to_all(sent_grads, "expert", split_axis=0, concat_axis=0, tiled=True)
    up_full, down_full, partial_grads = backward_part(
        inputs, got_grads, pre, act, up_local, down_local, owners, local_count, CAP
    )
    back_grads = lax.all_to_all(partial_grads, "expert", split_axis=0, concat_axis=0, tiled=True)
    up_grad = up_full.astype(jnp.bfloat16)
    down_grad = down_full.astype(jnp.bfloat16)
    returned = from_owners(back_out, copies, hidden_width).reshape(EXPERTS * CAP, hidden_width)
    summed_grads = from_owners(back_grads, copies, hidden_width).reshape(
        EXPERTS * CAP, hidden_width
    )
    weighted_rows = returned * slot_weight[:, None]
    mixed = jnp.dot(selection_index.T, weighted_rows, precision=upper_bound).astype(jnp.bfloat16)
    row_gradient = jnp.dot(selection_index.T, summed_grads, precision=upper_bound).astype(
        jnp.bfloat16
    )
    return (mixed, row_gradient, up_grad, down_grad)


def grad_kernel(a_ref, b_ref, o_ref):
    o_ref[...] = lax.dot_general(
        a_ref[0], b_ref[0], (((0,), (0,)), ((), ())), preferred_element_type=jnp.float32
    ).astype(o_ref.dtype)


def cost(local_count, slots, units, width):
    return pl.CostEstimate(
        flops=2 * local_count * slots * units * width,
        bytes_accessed=2 * local_count * (units * width + slots * (units + width)),
        transcendentals=0,
    )


def up_grad_call(inputs, pre_grad):
    local_count, slots, width = inputs.shape
    units = pre_grad.shape[2]
    tile = min(512, units)
    return pl.pallas_call(
        grad_kernel,
        grid=(local_count, units // tile),
        in_specs=[
            pl.BlockSpec((1, slots, width), lambda l, j: (l, 0, 0)),
            pl.BlockSpec((1, slots, tile), lambda l, j: (l, 0, j)),
        ],
        out_specs=pl.BlockSpec((width, tile), lambda l, j: (0, l * (units // tile) + j)),
        out_shape=jax.ShapeDtypeStruct((width, local_count * units), jnp.bfloat16),
        cost_estimate=cost(local_count, slots, units, width),
    )(inputs, pre_grad)


def down_grad_call(act, scaled):
    local_count, slots, width = scaled.shape
    units = act.shape[2]
    tile = min(512, units)
    return pl.pallas_call(
        grad_kernel,
        grid=(local_count, units // tile),
        in_specs=[
            pl.BlockSpec((1, slots, tile), lambda l, j: (l, 0, j)),
            pl.BlockSpec((1, slots, width), lambda l, j: (l, 0, 0)),
        ],
        out_specs=pl.BlockSpec((tile, width), lambda l, j: (l * (units // tile) + j, 0)),
        out_shape=jax.ShapeDtypeStruct((local_count * units, width), jnp.bfloat16),
        cost_estimate=cost(local_count, slots, units, width),
    )(act, scaled)


def dot_nt(a, b):
    return lax.dot_general(a, b, (((1,), (1,)), ((), ())), preferred_element_type=jnp.float32)


def dot_tn(a, b):
    return lax.dot_general(a, b, (((0,), (0,)), ((), ())), preferred_element_type=jnp.float32)


def slot_places(counts, order, mix_flat, me, line, local_count, pad, row_total, width):
    firsts = jnp.cumsum(counts) - counts
    matches = order[None, :] == jnp.arange(EXPERTS, dtype=jnp.int32)[:, None]
    count_of = jnp.sum(jnp.where(matches, jnp.repeat(counts, K)[None], 0), axis=1)
    first_of = jnp.sum(jnp.where(matches, jnp.repeat(firsts, K)[None], 0), axis=1)
    weight_of = jnp.sum(jnp.where(matches, mix_flat[None], 0.0), axis=1)
    lane = jnp.arange(width, dtype=jnp.int32)
    member, inner = lane // SPAN, lane % SPAN
    local, spot = inner // pad, inner % pad
    slot = spot - (me // PLANE) * CAP
    known = (member < PLANE) & (local < local_count) & (slot >= 0) & (slot < CAP)
    expert = (jnp.arange(line)[:, None] * PLANE + member[None]) * local_count + local[None]
    here = expert[:, :, None] == jnp.arange(EXPERTS, dtype=jnp.int32)
    spread = lambda v: jnp.sum(jnp.where(here, v[None, None], 0), axis=-1)
    filled = known[None] & (slot[None] < spread(count_of))
    target = jnp.where(filled, spread(first_of) + slot[None], -1).astype(jnp.float32)
    weight = jnp.where(filled, spread(weight_of), 0.0)
    high = lax.reduce_precision(weight, 8, 7)
    middle = lax.reduce_precision(weight - high, 8, 7)
    low = weight - high - middle
    return jnp.concatenate([target, high, middle, low]).astype(jnp.bfloat16)


def plane_kernel(
    line, local_count, pad,
    rows_ref, cot_ref, up_hbm, down_hbm,
    mixed_ref, part_ref, x_ref, s_ref, act_ref, pg_ref,
    rows_all, cot_all, up_ref, down_ref, sel, whi, wmid, wlo,
    x_send, s_send, o_send, d_send, o_got, d_got, pre_ref, acc_ref, m_send, m_got,
    w_sem, l_sem, r_ss, r_rs, c_ss, c_rs, x_ss, x_rs, s_ss, s_rs, o_ss, o_rs, d_ss, d_rs, m_ss, m_rs,
):
    me = lax.axis_index("expert")
    z, p = me // PLANE, lax.rem(me, PLANE)
    row_total, width = cot_ref.shape
    f32, bf16 = jnp.float32, jnp.bfloat16

    weights_in = [
        pltpu.make_async_copy(up_hbm, up_ref, w_sem.at[0]),
        pltpu.make_async_copy(down_hbm, down_ref, w_sem.at[1]),
    ]
    own = [
        pltpu.make_async_copy(rows_ref, rows_all.at[z], l_sem.at[0]),
        pltpu.make_async_copy(cot_ref, cot_all.at[z], l_sem.at[1]),
    ]
    for copy in own:
        copy.start()
    barrier = pltpu.get_barrier_semaphore()
    for k in range(1, PLANE):
        pl.semaphore_signal(barrier, inc=1, device_id={"expert": z * PLANE + lax.rem(p + k, PLANE)})
    for k in range(1, line):
        pl.semaphore_signal(barrier, inc=1, device_id={"expert": lax.rem(z + k, line) * PLANE + p})
    pl.semaphore_wait(barrier, PLANE - 1 + line - 1)
    for copy in own:
        copy.wait()
    for copy in weights_in:
        copy.start()

    def hop(buf, j, shift, ss, rs, lane):
        return pltpu.make_async_remote_copy(
            src_ref=buf.at[j], dst_ref=buf.at[j],
            send_sem=ss.at[lane, j], recv_sem=rs.at[j],
            device_id={"expert": lax.rem(me + (line + shift) * PLANE, line * PLANE)},
        )

    def pass_on(buf, j, shift, ss, rs):
        @pl.when((z + shift >= 0) & (z + shift < line))
        def _():
            hop(buf, j, shift, ss, rs, 0 if shift == 1 else 1).start()

    def settle(buf, ss, rs):
        for d in range(line):
            for shift in (1, -1):
                j = z - shift * d
                @pl.when((j >= 0) & (j < line) & (z + shift >= 0) & (z + shift < line))
                def _():
                    hop(buf, j, shift, ss, rs, 0 if shift == 1 else 1).wait_send()

    def gather_step(buf, d, ss, rs, after=None):
        for shift in (1, -1):
            j = z - shift * d
            @pl.when((j >= 0) & (j < line))
            def _():
                if d > 0:
                    hop(buf, j, shift, ss, rs, 0).wait_recv()
                pass_on(buf, j, shift, ss, rs)
            if after is not None:
                @pl.when(j == (0 if shift == 1 else line - 1))
                def _():
                    pass_on(after[0], z, shift, after[1], after[2])

    for d in range(line):
        gather_step(rows_all, d, r_ss, r_rs, (cot_all, c_ss, c_rs))

    for j in range(line):
        info = rows_all[j, row_total:, :].astype(f32)
        at = lax.broadcasted_iota(jnp.int32, info.shape, 0)
        pick = lambda q: jnp.sum(jnp.where(at == q * line + z, info, 0.0), axis=0, keepdims=True)
        hit = lax.broadcasted_iota(jnp.int32, (row_total, width), 0) == pick(0).astype(jnp.int32)
        block = pl.ds(j * row_total, row_total)
        sel[block, :] = jnp.where(hit, 1.0, 0.0).astype(bf16)
        for ref, q in ((whi, 1), (wmid, 2), (wlo, 3)):
            ref[block, :] = jnp.where(hit, pick(q), 0.0).astype(bf16)

    def swap(send, got, ss, rs, l, k):
        to = lax.rem(p + k, PLANE)
        return pltpu.make_async_remote_copy(
            src_ref=send.at[l, pl.ds(pl.multiple_of(to * pad, 16), pad)],
            dst_ref=got.at[l, pl.ds(pl.multiple_of(p * pad, 16), pad)],
            send_sem=ss.at[l, k], recv_sem=rs.at[l, k],
            device_id={"expert": z * PLANE + to},
        )

    def keep(send, got, rs, l):
        place = pl.ds(pl.multiple_of(p * pad, 16), pad)
        return pltpu.make_async_copy(send.at[l, place], got.at[l, place], rs.at[l, 0])

    def swap_start(send, got, ss, rs, l):
        for k in range(1, PLANE):
            swap(send, got, ss, rs, l, k).start()
        keep(send, got, rs, l).start()

    def swap_wait(send, got, ss, rs, l):
        for k in range(1, PLANE):
            swap(send, got, ss, rs, l, k).wait()
        keep(send, got, rs, l).wait()

    def dispatch(values, refs, send, got, ss, rs):
        for q in range(PLANE):
            lanes = pl.ds(q * SPAN, SPAN)
            picked = sum(dot_tn(ref[:, lanes], values) for ref in refs).astype(bf16)
            for l in range(local_count):
                send[l, q * pad : (q + 1) * pad, :] = picked[l * pad : (l + 1) * pad]
        for l in range(local_count):
            swap_start(send, got, ss, rs, l)

    dispatch(
        rows_all[:, :row_total, :].reshape(line * row_total, width), [sel], x_send, x_ref, x_ss, x_rs
    )
    for d in range(1, line):
        gather_step(cot_all, d, c_ss, c_rs)
    dispatch(
        cot_all[...].reshape(line * row_total, width), [whi, wmid, wlo], s_send, s_ref, s_ss, s_rs
    )
    for copy in weights_in:
        copy.wait()

    for l in range(local_count):
        swap_wait(x_send, x_ref, x_ss, x_rs, l)
        acc_ref[...] = jnp.zeros_like(acc_ref)

        @pl.loop(0, FF // TILE)
        def _(f):
            own_units = pl.ds(pl.multiple_of(f * TILE, TILE), TILE)
            units = pl.ds(pl.multiple_of(l * FF + f * TILE, TILE), TILE)
            pre = jnp.dot(x_ref[l], up_ref[:, units], preferred_element_type=f32)
            act = (pre / (1.0 + jnp.exp(-pre))).astype(bf16)
            pre_ref[l, :, own_units] = pre
            act_ref[l, :, own_units] = act
            acc_ref[...] += jnp.dot(act, down_ref[units, :], preferred_element_type=f32)

        o_send[l] = acc_ref[...].astype(bf16)
        swap_start(o_send, o_got, o_ss, o_rs, l)

    def back(l):
        swap_wait(s_send, s_ref, s_ss, s_rs, l)
        acc_ref[...] = jnp.zeros_like(acc_ref)

        @pl.loop(0, FF // TILE)
        def _(f):
            own_units = pl.ds(pl.multiple_of(f * TILE, TILE), TILE)
            units = pl.ds(pl.multiple_of(l * FF + f * TILE, TILE), TILE)
            act_grad = dot_nt(s_ref[l], down_ref[units, :])
            pre = pre_ref[l, :, own_units]
            sg = 1.0 / (1.0 + jnp.exp(-pre))
            pre_grad = (act_grad * sg * (1.0 + pre * (1.0 - sg))).astype(bf16)
            pg_ref[l, :, own_units] = pre_grad
            acc_ref[...] += dot_nt(pre_grad, up_ref[:, units])

        d_send[l] = acc_ref[...].astype(bf16)
        swap_start(d_send, d_got, d_ss, d_rs, l)

    def combined(got, refs, j):
        block = pl.ds(j * row_total, row_total)
        total = jnp.zeros((row_total, width), f32)
        for q in range(PLANE):
            slots = jnp.concatenate(
                [got[l, q * pad : (q + 1) * pad, :] for l in range(local_count)]
                + [jnp.zeros((SPAN - local_count * pad, width), bf16)],
                axis=0,
            )
            for ref in refs:
                total += jnp.dot(ref[block, pl.ds(q * SPAN, SPAN)], slots, preferred_element_type=f32)
        return total

    def home(k):
        to = lax.rem(z + k, line)
        return pltpu.make_async_remote_copy(
            src_ref=m_send.at[to], dst_ref=m_got.at[z],
            send_sem=m_ss.at[k], recv_sem=m_rs.at[k],
            device_id={"expert": to * PLANE + p},
        )

    back(0)
    for l in range(local_count):
        swap_wait(o_send, o_got, o_ss, o_rs, l)
    for j in range(line):
        m_send[j] = combined(o_got, [whi, wmid], j).astype(bf16)
    for k in range(1, line):
        home(k).start()
    keep_mixed = pltpu.make_async_copy(m_send.at[z], m_got.at[z], m_rs.at[0])
    keep_mixed.start()
    for l in range(1, local_count):
        back(l)
    for l in range(local_count):
        swap_wait(d_send, d_got, d_ss, d_rs, l)
    for j in range(line):
        part_ref[j] = combined(d_got, [sel], j).astype(bf16)
    for k in range(1, line):
        home(k).wait()
    keep_mixed.wait()
    mixed_ref[...] = sum(m_got[j].astype(f32) for j in range(line)).astype(bf16)
    settle(rows_all, r_ss, r_rs)
    settle(cot_all, c_ss, c_rs)


def plane_call(rows, cotangent, up_proj, down_proj, line, local_count, pad):
    bf16, f32 = jnp.bfloat16, jnp.float32
    row_total, width = cotangent.shape
    taken = PLANE * pad
    slots = (local_count, taken, width)
    wide = (local_count, taken, FF)
    dma = pltpu.SemaphoreType.DMA
    vmem, anywhere = pl.BlockSpec(memory_space=pltpu.VMEM), pl.BlockSpec(memory_space=pl.ANY)
    table = pltpu.VMEM((line * row_total, width), bf16)
    blocks = (line, row_total, width)
    swaps = (local_count, PLANE)
    return pl.pallas_call(
        functools.partial(plane_kernel, line, local_count, pad),
        out_shape=[
            jax.ShapeDtypeStruct((row_total, width), bf16),
            jax.ShapeDtypeStruct(blocks, bf16),
            jax.ShapeDtypeStruct(slots, bf16),
            jax.ShapeDtypeStruct(slots, bf16),
            jax.ShapeDtypeStruct(wide, bf16),
            jax.ShapeDtypeStruct(wide, bf16),
        ],
        in_specs=[vmem, vmem, anywhere, anywhere],
        out_specs=[vmem] * 6,
        scratch_shapes=[
            pltpu.VMEM((line,) + rows.shape, bf16),
            pltpu.VMEM(blocks, bf16),
            pltpu.VMEM(up_proj.shape, bf16),
            pltpu.VMEM(down_proj.shape, bf16),
        ]
        + [table] * 4
        + [pltpu.VMEM(slots, bf16)] * 6
        + [pltpu.VMEM(wide, f32), pltpu.VMEM((taken, width), f32)]
        + [pltpu.VMEM(blocks, bf16)] * 2
        + [dma((2,)), dma((2,))]
        + [dma((2, line)), dma((line,))] * 2
        + [dma(swaps)] * 8
        + [dma((line,))] * 2,
        compiler_params=pltpu.CompilerParams(
            collective_id=0, has_side_effects=True, vmem_limit_bytes=60 << 20
        ),
    )(rows, cotangent, up_proj, down_proj)


def plane_plan(rows, cotangent, up_proj, down_proj, mix_weight, task_counts, expert_order):
    owners = lax.axis_size("expert")
    me = lax.axis_index("expert")
    line = owners // PLANE
    row_total, width = rows.shape
    local_count = up_proj.shape[1] // FF
    pad = (line * CAP + 15) // 16 * 16
    places = slot_places(
        task_counts[0], expert_order[0], mix_weight.reshape(-1),
        me, line, local_count, pad, row_total, width,
    )
    mixed, parts, inputs, scaled, act, pre_grad = plane_call(
        jnp.concatenate([rows, places]), cotangent, up_proj, down_proj, line, local_count, pad
    )
    groups = [[z * PLANE + p for z in range(line)] for p in range(PLANE)]
    home = lax.all_to_all(parts, "expert", 0, 0, axis_index_groups=groups, tiled=True)
    up_grad = up_grad_call(inputs, pre_grad)
    down_grad = down_grad_call(act, scaled)
    row_gradient = jnp.sum(home.astype(jnp.float32), axis=0).astype(jnp.bfloat16)
    return (mixed, row_gradient, up_grad, down_grad)


def per_device(rows, cotangent, up_proj, *others):
    owners = lax.axis_size("expert")
    whole_experts = up_proj.shape[1] % FF == 0
    local_count = up_proj.shape[1] // FF
    fits = owners % PLANE == 0 and local_count * (-(-owners // PLANE * CAP // 16) * 16) <= SPAN
    wide_plane = fits and owners > PLANE and rows.shape[1] == PLANE * SPAN
    plan = plane_plan if whole_experts and wide_plane else direct_plan
    return plan(rows, cotangent, up_proj, *others)


def solution(mesh):
    return jax.shard_map(
        per_device,
        mesh=mesh,
        in_specs=(
            P(("group", "expert"), None),
            P(("group", "expert"), None),
            P(None, "expert"),
            P("expert", None),
            P(),
            P(("group", "expert"), None),
            P(("group", "expert"), None),
        ),
        out_specs=(
            P(("group", "expert"), None),
            P(("group", "expert"), None),
            P("group", "expert"),
            P("expert", "group"),
        ),
        check_vma=False,
    )
```

```python
import functools

import jax
import jax.numpy as jnp
from jax import lax
from jax.experimental import pallas as pl
from jax.experimental.pallas import tpu as pltpu
from jax.sharding import PartitionSpec as P

FF = 2048
EXPERTS = 32
TASKS = 8
K = 4
CAP = 18
PLANE = 4
TILE = 512


def block_route(counts, expert_list, mix_flat, row_total):
    firsts = jnp.cumsum(counts) - counts
    labels = jnp.arange(EXPERTS, dtype=jnp.int32)
    matches = expert_list[None, :] == labels[:, None]
    position = jnp.sum(jnp.where(matches, labels[None, :], 0), axis=1)
    task_of = position // K
    task_match = task_of[:, None] == jnp.arange(TASKS, dtype=jnp.int32)[None, :]
    count_of = jnp.sum(jnp.where(task_match, counts[None, :], 0), axis=1)
    first_of = jnp.sum(jnp.where(task_match, firsts[None, :], 0), axis=1)
    weight_of = jnp.sum(
        jnp.where(matches, mix_flat[None, :], jnp.zeros_like(mix_flat)[None, :]), axis=1
    )
    slot_index = jnp.arange(CAP, dtype=jnp.int32)
    filled = slot_index[None, :] < count_of[:, None]
    targets = first_of[:, None] + slot_index[None, :]
    row_index = jnp.arange(row_total, dtype=jnp.int32)
    selection_index = (targets[:, :, None] == row_index[None, None, :]) & filled[:, :, None]
    selection_index = selection_index.reshape(EXPERTS * CAP, row_total).astype(jnp.float32)
    slot_weight = jnp.where(filled, weight_of[:, None], jnp.zeros_like(weight_of)[:, None]).reshape(
        -1
    )
    return (selection_index, slot_weight)


def to_owners(values, copies, owners):
    if copies > 1:
        return jnp.repeat(values, copies, axis=0)
    return values.reshape((owners, -1) + values.shape[2:])


def from_owners(values, copies, hidden_width):
    if copies > 1:
        return jnp.sum(values.reshape(EXPERTS, copies, CAP, hidden_width), axis=1)
    return values.reshape(EXPERTS, CAP, hidden_width)


def forward_part(got_rows, up_local, down_local, owners, local_count, slot_count):
    hidden_width = got_rows.shape[-1]
    inputs = got_rows.reshape(owners, local_count, slot_count, hidden_width)
    pre = jnp.einsum("nlcd,dlf->nlcf", inputs, up_local, preferred_element_type=jnp.float32)
    act = jax.nn.silu(pre).astype(jnp.bfloat16)
    outputs = jnp.einsum("nlcf,lfd->nlcd", act, down_local, preferred_element_type=jnp.float32)
    return (inputs, pre, act, outputs.reshape(owners, local_count * slot_count, hidden_width))


def backward_part(
    inputs, got_grads, pre, act, up_local, down_local, owners, local_count, slot_count
):
    hidden_width = inputs.shape[-1]
    scaled = got_grads.reshape(owners, local_count, slot_count, hidden_width)
    act_grad = jnp.einsum("nlcd,lfd->nlcf", scaled, down_local, preferred_element_type=jnp.float32)
    sigmoid = jax.nn.sigmoid(pre)
    pre_grad = (act_grad * sigmoid * (1.0 + pre * (1.0 - sigmoid))).astype(jnp.bfloat16)
    down_grad = jnp.einsum("nlcf,nlcd->lfd", act, scaled, preferred_element_type=jnp.float32)
    up_grad = jnp.einsum("nlcd,nlcf->dlf", inputs, pre_grad, preferred_element_type=jnp.float32)
    partial_grads = jnp.einsum(
        "nlcf,dlf->nlcd", pre_grad, up_local, preferred_element_type=jnp.float32
    )
    units = up_local.shape[1] * up_local.shape[2]
    return (
        up_grad.reshape(hidden_width, units),
        down_grad.reshape(units, hidden_width),
        partial_grads.reshape(owners, local_count * slot_count, hidden_width),
    )


def direct_plan(rows, cotangent, up_proj, down_proj, mix_weight, task_counts, expert_order):
    owners = lax.axis_size("expert")
    row_total = rows.shape[0]
    hidden_width = rows.shape[1]
    units = up_proj.shape[1]
    local_units = min(units, FF)
    local_count = max(units // FF, 1)
    copies = max(FF // units, 1)
    selection_index, slot_weight = block_route(
        task_counts[0], expert_order[0], mix_weight.reshape(-1), row_total
    )
    select_half = selection_index.astype(jnp.bfloat16)
    slot_row_values = jnp.dot(select_half, rows, preferred_element_type=jnp.float32).astype(
        jnp.bfloat16
    )
    slot_gradient_rows = jnp.dot(select_half, cotangent, preferred_element_type=jnp.float32)
    scaled = (slot_weight[:, None] * slot_gradient_rows).astype(jnp.bfloat16)
    upper_bound = lax.Precision.HIGHEST
    sent_rows = to_owners(slot_row_values.reshape(EXPERTS, CAP, hidden_width), copies, owners)
    sent_grads = to_owners(scaled.reshape(EXPERTS, CAP, hidden_width), copies, owners)
    up_local = up_proj.reshape(hidden_width, local_count, local_units)
    down_local = down_proj.reshape(local_count, local_units, hidden_width)
    got_rows = lax.all_to_all(sent_rows, "expert", split_axis=0, concat_axis=0, tiled=True)
    inputs, pre, act, outputs = forward_part(
        got_rows, up_local, down_local, owners, local_count, CAP
    )
    back_out = lax.all_to_all(outputs, "expert", split_axis=0, concat_axis=0, tiled=True)
    got_grads = lax.all_to_all(sent_grads, "expert", split_axis=0, concat_axis=0, tiled=True)
    up_full, down_full, partial_grads = backward_part(
        inputs, got_grads, pre, act, up_local, down_local, owners, local_count, CAP
    )
    back_grads = lax.all_to_all(partial_grads, "expert", split_axis=0, concat_axis=0, tiled=True)
    up_grad = up_full.astype(jnp.bfloat16)
    down_grad = down_full.astype(jnp.bfloat16)
    returned = from_owners(back_out, copies, hidden_width).reshape(EXPERTS * CAP, hidden_width)
    summed_grads = from_owners(back_grads, copies, hidden_width).reshape(
        EXPERTS * CAP, hidden_width
    )
    weighted_rows = returned * slot_weight[:, None]
    mixed = jnp.dot(selection_index.T, weighted_rows, precision=upper_bound).astype(jnp.bfloat16)
    row_gradient = jnp.dot(selection_index.T, summed_grads, precision=upper_bound).astype(
        jnp.bfloat16
    )
    return (mixed, row_gradient, up_grad, down_grad)


def grad_kernel(a_ref, b_ref, o_ref):
    o_ref[...] = lax.dot_general(
        a_ref[0], b_ref[0], (((0,), (0,)), ((), ())), preferred_element_type=jnp.float32
    ).astype(o_ref.dtype)


def cost(local_count, slots, units, width):
    return pl.CostEstimate(
        flops=2 * local_count * slots * units * width,
        bytes_accessed=2 * local_count * (units * width + slots * (units + width)),
        transcendentals=0,
    )


def up_grad_call(inputs, pre_grad):
    local_count, slots, width = inputs.shape
    units = pre_grad.shape[2]
    tile = min(512, units)
    return pl.pallas_call(
        grad_kernel,
        grid=(local_count, units // tile),
        in_specs=[
            pl.BlockSpec((1, slots, width), lambda l, j: (l, 0, 0)),
            pl.BlockSpec((1, slots, tile), lambda l, j: (l, 0, j)),
        ],
        out_specs=pl.BlockSpec((width, tile), lambda l, j: (0, l * (units // tile) + j)),
        out_shape=jax.ShapeDtypeStruct((width, local_count * units), jnp.bfloat16),
        cost_estimate=cost(local_count, slots, units, width),
    )(inputs, pre_grad)


def down_grad_call(act, scaled):
    local_count, slots, width = scaled.shape
    units = act.shape[2]
    tile = min(512, units)
    return pl.pallas_call(
        grad_kernel,
        grid=(local_count, units // tile),
        in_specs=[
            pl.BlockSpec((1, slots, tile), lambda l, j: (l, 0, j)),
            pl.BlockSpec((1, slots, width), lambda l, j: (l, 0, 0)),
        ],
        out_specs=pl.BlockSpec((tile, width), lambda l, j: (l * (units // tile) + j, 0)),
        out_shape=jax.ShapeDtypeStruct((local_count * units, width), jnp.bfloat16),
        cost_estimate=cost(local_count, slots, units, width),
    )(act, scaled)


def dot_nt(a, b):
    return lax.dot_general(a, b, (((1,), (1,)), ((), ())), preferred_element_type=jnp.float32)


def dot_tn(a, b):
    return lax.dot_general(a, b, (((0,), (0,)), ((), ())), preferred_element_type=jnp.float32)


def slot_places(counts, order, mix_flat, me, line, local_count, pad, row_total, width):
    task = jnp.arange(TASKS)
    firsts = jnp.sum(jnp.where(task[None, :] < task[:, None], counts[None, :], 0), axis=1)
    matches = order[None, :] == jnp.arange(EXPERTS, dtype=jnp.int32)[:, None]
    count_of = jnp.sum(jnp.where(matches, jnp.repeat(counts, K)[None], 0), axis=1)
    first_of = jnp.sum(jnp.where(matches, jnp.repeat(firsts, K)[None], 0), axis=1)
    weight_of = jnp.sum(jnp.where(matches, mix_flat[None], 0.0), axis=1)
    lane = jnp.arange(width, dtype=jnp.int32)
    member, local, spot = lane // pad % PLANE, lane // pad // PLANE, lane % pad
    slot = spot - (me // PLANE) * CAP
    known = (local < local_count) & (slot >= 0) & (slot < CAP)
    expert = (jnp.arange(line)[:, None] * PLANE + member[None]) * local_count + local[None]
    here = expert[:, :, None] == jnp.arange(EXPERTS, dtype=jnp.int32)
    spread = lambda v: jnp.sum(jnp.where(here, v[None, None], 0), axis=-1)
    filled = known[None] & (slot[None] < spread(count_of))
    target = jnp.where(filled, spread(first_of) + slot[None], -1).astype(jnp.float32)
    weight = jnp.where(filled, spread(weight_of), 0.0)
    high = lax.reduce_precision(weight, 8, 7)
    middle = lax.reduce_precision(weight - high, 8, 7)
    low = weight - high - middle
    return jnp.concatenate([target, high, middle, low]).astype(jnp.bfloat16)


def plane_kernel(
    line, local_count, pad,
    rows_ref, places_ref, cot_ref, up_hbm, down_hbm,
    mixed_ref, part_ref, x_out, s_out, act_out, pg_out,
    rows_all, cot_all, up_ref, down_ref, sel, w_ref, x_ref, s_ref, act_ref, pg_ref,
    x_send, s_send, o_send, d_send, o_got, d_got, pre_ref, acc_ref, m_send, m_got,
    w_sem, l_sem, out_sem, r_ss, r_rs, c_ss, c_rs, x_ss, x_rs, s_ss, s_rs, o_ss, o_rs, d_ss, d_rs, m_ss, m_rs,
):
    me = lax.axis_index("expert")
    z, p = me // PLANE, lax.rem(me, PLANE)
    row_total, width = cot_ref.shape
    f32, bf16 = jnp.float32, jnp.bfloat16

    weights_in = [
        pltpu.make_async_copy(up_hbm, up_ref, w_sem.at[0]),
        pltpu.make_async_copy(down_hbm, down_ref, w_sem.at[1]),
    ]
    own = [
        pltpu.make_async_copy(rows_ref, rows_all.at[z, pl.ds(0, row_total)], l_sem.at[0]),
        pltpu.make_async_copy(cot_ref, cot_all.at[z], l_sem.at[1]),
        pltpu.make_async_copy(
            places_ref, rows_all.at[z, pl.ds(row_total, places_ref.shape[0])], l_sem.at[2]
        ),
    ]
    for copy in own:
        copy.start()
    barrier = pltpu.get_barrier_semaphore()
    for k in range(1, PLANE):
        pl.semaphore_signal(barrier, inc=1, device_id={"expert": z * PLANE + lax.rem(p + k, PLANE)})
    for k in range(1, line):
        pl.semaphore_signal(barrier, inc=1, device_id={"expert": lax.rem(z + k, line) * PLANE + p})
    pl.semaphore_wait(barrier, PLANE - 1 + line - 1)
    for copy in own:
        copy.wait()
    for copy in weights_in:
        copy.start()

    def hop(buf, j, shift, ss, rs, lane):
        return pltpu.make_async_remote_copy(
            src_ref=buf.at[j], dst_ref=buf.at[j],
            send_sem=ss.at[lane, j], recv_sem=rs.at[j],
            device_id={"expert": lax.rem(me + (line + shift) * PLANE, line * PLANE)},
        )

    def pass_on(buf, j, shift, ss, rs):
        @pl.when((z + shift >= 0) & (z + shift < line))
        def _():
            hop(buf, j, shift, ss, rs, 0 if shift == 1 else 1).start()

    def settle(buf, ss, rs):
        for d in range(line):
            for shift in (1, -1):
                j = z - shift * d
                @pl.when((j >= 0) & (j < line) & (z + shift >= 0) & (z + shift < line))
                def _():
                    hop(buf, j, shift, ss, rs, 0 if shift == 1 else 1).wait_send()

    def gather_step(buf, d, ss, rs, after=None):
        for shift in (1, -1):
            j = z - shift * d
            @pl.when((j >= 0) & (j < line))
            def _():
                if d > 0:
                    hop(buf, j, shift, ss, rs, 0).wait_recv()
                pass_on(buf, j, shift, ss, rs)
            if after is not None:
                @pl.when(j == (0 if shift == 1 else line - 1))
                def _():
                    pass_on(after[0], z, shift, after[1], after[2])

    for d in range(line):
        gather_step(rows_all, d, r_ss, r_rs, (cot_all, c_ss, c_rs))

    lanes = sel.shape[1]
    weight = jnp.zeros((1, lanes), f32)
    for j in range(line):
        info = rows_all[j, row_total:, :lanes].astype(f32)
        at = lax.broadcasted_iota(jnp.int32, info.shape, 0)
        pick = lambda q: jnp.sum(jnp.where(at == q * line + z, info, 0.0), axis=0, keepdims=True)
        hit = lax.broadcasted_iota(jnp.int32, (row_total, lanes), 0) == pick(0).astype(jnp.int32)
        sel[j * row_total : (j + 1) * row_total, :] = jnp.where(hit, 1.0, 0.0).astype(bf16)
        weight += pick(1) + pick(2) + pick(3)
    w_ref[...] = jnp.transpose(jnp.broadcast_to(weight, (w_ref.shape[1], lanes)))

    def swap(send, got, ss, rs, l, k):
        to = lax.rem(p + k, PLANE)
        return pltpu.make_async_remote_copy(
            src_ref=send.at[l, pl.ds(pl.multiple_of(to * pad, 16), pad)],
            dst_ref=got.at[l, pl.ds(pl.multiple_of(p * pad, 16), pad)],
            send_sem=ss.at[l, k], recv_sem=rs.at[l, k],
            device_id={"expert": z * PLANE + to},
        )

    def keep(send, got, rs, l):
        place = pl.ds(pl.multiple_of(p * pad, 16), pad)
        return pltpu.make_async_copy(send.at[l, place], got.at[l, place], rs.at[l, 0])

    def swap_start(send, got, ss, rs, l):
        for k in range(1, PLANE):
            swap(send, got, ss, rs, l, k).start()
        keep(send, got, rs, l).start()

    def swap_wait(send, got, ss, rs, l):
        for k in range(1, PLANE):
            swap(send, got, ss, rs, l, k).wait()
        keep(send, got, rs, l).wait()

    taken = PLANE * pad

    def leave(ref, out, n, l):
        return pltpu.make_async_copy(ref.at[l], out.at[l], out_sem.at[n, l])

    def dispatch(values, scale, send, got, ss, rs):
        picked = dot_tn(sel[...], values)
        if scale is not None:
            picked = scale * picked
        picked = picked.astype(bf16)
        for l in range(local_count):
            send[l] = picked[l * taken : (l + 1) * taken]
        for l in range(local_count):
            swap_start(send, got, ss, rs, l)

    def forward(l):
        swap_wait(x_send, x_ref, x_ss, x_rs, l)
        leave(x_ref, x_out, 0, l).start()
        acc_ref[...] = jnp.zeros_like(acc_ref)

        @pl.loop(0, FF // TILE)
        def _(f):
            own_units = pl.ds(pl.multiple_of(f * TILE, TILE), TILE)
            units = pl.ds(pl.multiple_of(l * FF + f * TILE, TILE), TILE)
            pre = jnp.dot(x_ref[l], up_ref[:, units], preferred_element_type=f32)
            act = (pre / (1.0 + jnp.exp(-pre))).astype(bf16)
            pre_ref[l, :, own_units] = pre
            act_ref[l, :, own_units] = act
            acc_ref[...] += jnp.dot(act, down_ref[units, :], preferred_element_type=f32)

        o_send[l] = acc_ref[...].astype(bf16)
        swap_start(o_send, o_got, o_ss, o_rs, l)
        leave(act_ref, act_out, 2, l).start()

    dispatch(
        rows_all[:, :row_total, :].reshape(line * row_total, width), None, x_send, x_ref, x_ss, x_rs
    )
    for d in range(1, line - 1):
        gather_step(cot_all, d, c_ss, c_rs)
    for copy in weights_in:
        copy.wait()
    forward(0)
    gather_step(cot_all, line - 1, c_ss, c_rs)
    dispatch(
        cot_all[...].reshape(line * row_total, width), w_ref[:, :1], s_send, s_ref, s_ss, s_rs
    )
    for l in range(1, local_count):
        forward(l)

    def back(l):
        swap_wait(s_send, s_ref, s_ss, s_rs, l)
        leave(s_ref, s_out, 1, l).start()
        acc_ref[...] = jnp.zeros_like(acc_ref)

        @pl.loop(0, FF // TILE)
        def _(f):
            own_units = pl.ds(pl.multiple_of(f * TILE, TILE), TILE)
            units = pl.ds(pl.multiple_of(l * FF + f * TILE, TILE), TILE)
            act_grad = dot_nt(s_ref[l], down_ref[units, :])
            pre = pre_ref[l, :, own_units]
            sg = 1.0 / (1.0 + jnp.exp(-pre))
            pre_grad = (act_grad * sg * (1.0 + pre * (1.0 - sg))).astype(bf16)
            pg_ref[l, :, own_units] = pre_grad
            acc_ref[...] += dot_nt(pre_grad, up_ref[:, units])

        d_send[l] = acc_ref[...].astype(bf16)
        swap_start(d_send, d_got, d_ss, d_rs, l)
        leave(pg_ref, pg_out, 3, l).start()

    def combined(slots):
        total = jnp.dot(sel[...], slots, preferred_element_type=f32)
        return total.astype(bf16).reshape(line, row_total, width)

    def home(k):
        to = lax.rem(z + k, line)
        return pltpu.make_async_remote_copy(
            src_ref=m_send.at[to], dst_ref=m_got.at[z],
            send_sem=m_ss.at[k], recv_sem=m_rs.at[k],
            device_id={"expert": to * PLANE + p},
        )

    back(0)
    for l in range(local_count):
        swap_wait(o_send, o_got, o_ss, o_rs, l)
    outs = o_got[...].reshape(lanes, width).astype(f32)
    m_send[...] = combined((w_ref[:, :1] * outs).astype(bf16))
    for k in range(1, line):
        home(k).start()
    keep_mixed = pltpu.make_async_copy(m_send.at[z], m_got.at[z], m_rs.at[0])
    keep_mixed.start()
    for l in range(1, local_count):
        back(l)
    for l in range(local_count):
        swap_wait(d_send, d_got, d_ss, d_rs, l)
    part_ref[...] = combined(d_got[...].reshape(lanes, width))
    for k in range(1, line):
        home(k).wait()
    keep_mixed.wait()
    mixed_ref[...] = sum(m_got[j].astype(f32) for j in range(line)).astype(bf16)
    settle(rows_all, r_ss, r_rs)
    settle(cot_all, c_ss, c_rs)
    for l in range(local_count):
        for n, (ref, out) in enumerate(
            ((x_ref, x_out), (s_ref, s_out), (act_ref, act_out), (pg_ref, pg_out))
        ):
            leave(ref, out, n, l).wait()


def plane_call(rows, places, cotangent, up_proj, down_proj, line, local_count, pad):
    bf16, f32 = jnp.bfloat16, jnp.float32
    row_total, width = cotangent.shape
    taken = PLANE * pad
    slots = (local_count, taken, width)
    wide = (local_count, taken, FF)
    dma = pltpu.SemaphoreType.DMA
    vmem, anywhere = pl.BlockSpec(memory_space=pltpu.VMEM), pl.BlockSpec(memory_space=pl.ANY)
    lanes = local_count * taken
    blocks = (line, row_total, width)
    swaps = (local_count, PLANE)
    return pl.pallas_call(
        functools.partial(plane_kernel, line, local_count, pad),
        out_shape=[
            jax.ShapeDtypeStruct((row_total, width), bf16),
            jax.ShapeDtypeStruct(blocks, bf16),
            jax.ShapeDtypeStruct(slots, bf16),
            jax.ShapeDtypeStruct(slots, bf16),
            jax.ShapeDtypeStruct(wide, bf16),
            jax.ShapeDtypeStruct(wide, bf16),
        ],
        in_specs=[vmem, vmem, vmem, anywhere, anywhere],
        out_specs=[vmem] * 2 + [anywhere] * 4,
        scratch_shapes=[
            pltpu.VMEM((line, row_total + places.shape[0], width), bf16),
            pltpu.VMEM(blocks, bf16),
            pltpu.VMEM(up_proj.shape, bf16),
            pltpu.VMEM(down_proj.shape, bf16),
        ]
        + [pltpu.VMEM((line * row_total, lanes), bf16), pltpu.VMEM((lanes, 128), f32)]
        + [pltpu.VMEM(slots, bf16)] * 2
        + [pltpu.VMEM(wide, bf16)] * 2
        + [pltpu.VMEM(slots, bf16)] * 6
        + [pltpu.VMEM(wide, f32), pltpu.VMEM((taken, width), f32)]
        + [pltpu.VMEM(blocks, bf16)] * 2
        + [dma((2,)), dma((3,)), dma((4, local_count))]
        + [dma((2, line)), dma((line,))] * 2
        + [dma(swaps)] * 8
        + [dma((line,))] * 2,
        compiler_params=pltpu.CompilerParams(
            collective_id=0, has_side_effects=True, vmem_limit_bytes=60 << 20
        ),
    )(rows, places, cotangent, up_proj, down_proj)


def plane_plan(rows, cotangent, up_proj, down_proj, mix_weight, task_counts, expert_order):
    owners = lax.axis_size("expert")
    me = lax.axis_index("expert")
    line = owners // PLANE
    row_total, width = rows.shape
    local_count = up_proj.shape[1] // FF
    pad = (line * CAP + 15) // 16 * 16
    places = slot_places(
        task_counts[0], expert_order[0], mix_weight.reshape(-1),
        me, line, local_count, pad, row_total, width,
    )
    mixed, parts, inputs, scaled, act, pre_grad = plane_call(
        rows, places, cotangent, up_proj, down_proj, line, local_count, pad
    )
    groups = [[z * PLANE + p for z in range(line)] for p in range(PLANE)]
    home = lax.all_to_all(parts, "expert", 0, 0, axis_index_groups=groups, tiled=True)
    up_grad = up_grad_call(inputs, pre_grad)
    down_grad = down_grad_call(act, scaled)
    row_gradient = jnp.sum(home.astype(jnp.float32), axis=0).astype(jnp.bfloat16)
    return (mixed, row_gradient, up_grad, down_grad)


def per_device(rows, cotangent, up_proj, *others):
    owners = lax.axis_size("expert")
    whole_experts = up_proj.shape[1] % FF == 0
    local_count = up_proj.shape[1] // FF
    fits = owners % PLANE == 0 and local_count * -(-owners // PLANE * CAP // 16) * 16 * PLANE <= rows.shape[1]
    wide_plane = fits and owners > PLANE
    plan = plane_plan if whole_experts and wide_plane else direct_plan
    return plan(rows, cotangent, up_proj, *others)


def solution(mesh):
    return jax.shard_map(
        per_device,
        mesh=mesh,
        in_specs=(
            P(("group", "expert"), None),
            P(("group", "expert"), None),
            P(None, "expert"),
            P("expert", None),
            P(),
            P(("group", "expert"), None),
            P(("group", "expert"), None),
        ),
        out_specs=(
            P(("group", "expert"), None),
            P(("group", "expert"), None),
            P("group", "expert"),
            P("expert", "group"),
        ),
        check_vma=False,
    )
```

```python
import functools

import jax
import jax.numpy as jnp
from jax import lax
from jax.experimental import pallas as pl
from jax.experimental.pallas import tpu as pltpu
from jax.sharding import PartitionSpec as P

FF = 2048
EXPERTS = 32
TASKS = 8
K = 4
CAP = 18
PLANE = 4
TILE = 1024


def block_route(counts, expert_list, mix_flat, row_total):
    firsts = jnp.cumsum(counts) - counts
    labels = jnp.arange(EXPERTS, dtype=jnp.int32)
    matches = expert_list[None, :] == labels[:, None]
    position = jnp.sum(jnp.where(matches, labels[None, :], 0), axis=1)
    task_of = position // K
    task_match = task_of[:, None] == jnp.arange(TASKS, dtype=jnp.int32)[None, :]
    count_of = jnp.sum(jnp.where(task_match, counts[None, :], 0), axis=1)
    first_of = jnp.sum(jnp.where(task_match, firsts[None, :], 0), axis=1)
    weight_of = jnp.sum(
        jnp.where(matches, mix_flat[None, :], jnp.zeros_like(mix_flat)[None, :]), axis=1
    )
    slot_index = jnp.arange(CAP, dtype=jnp.int32)
    filled = slot_index[None, :] < count_of[:, None]
    targets = first_of[:, None] + slot_index[None, :]
    row_index = jnp.arange(row_total, dtype=jnp.int32)
    selection_index = (targets[:, :, None] == row_index[None, None, :]) & filled[:, :, None]
    selection_index = selection_index.reshape(EXPERTS * CAP, row_total).astype(jnp.float32)
    slot_weight = jnp.where(filled, weight_of[:, None], jnp.zeros_like(weight_of)[:, None]).reshape(
        -1
    )
    return (selection_index, slot_weight)


def to_owners(values, copies, owners):
    if copies > 1:
        return jnp.repeat(values, copies, axis=0)
    return values.reshape((owners, -1) + values.shape[2:])


def from_owners(values, copies, hidden_width):
    if copies > 1:
        return jnp.sum(values.reshape(EXPERTS, copies, CAP, hidden_width), axis=1)
    return values.reshape(EXPERTS, CAP, hidden_width)


def forward_part(got_rows, up_local, down_local, owners, local_count, slot_count):
    hidden_width = got_rows.shape[-1]
    inputs = got_rows.reshape(owners, local_count, slot_count, hidden_width)
    pre = jnp.einsum("nlcd,dlf->nlcf", inputs, up_local, preferred_element_type=jnp.float32)
    act = jax.nn.silu(pre).astype(jnp.bfloat16)
    outputs = jnp.einsum("nlcf,lfd->nlcd", act, down_local, preferred_element_type=jnp.float32)
    return (inputs, pre, act, outputs.reshape(owners, local_count * slot_count, hidden_width))


def backward_part(
    inputs, got_grads, pre, act, up_local, down_local, owners, local_count, slot_count
):
    hidden_width = inputs.shape[-1]
    scaled = got_grads.reshape(owners, local_count, slot_count, hidden_width)
    act_grad = jnp.einsum("nlcd,lfd->nlcf", scaled, down_local, preferred_element_type=jnp.float32)
    sigmoid = jax.nn.sigmoid(pre)
    pre_grad = (act_grad * sigmoid * (1.0 + pre * (1.0 - sigmoid))).astype(jnp.bfloat16)
    down_grad = jnp.einsum("nlcf,nlcd->lfd", act, scaled, preferred_element_type=jnp.float32)
    up_grad = jnp.einsum("nlcd,nlcf->dlf", inputs, pre_grad, preferred_element_type=jnp.float32)
    partial_grads = jnp.einsum(
        "nlcf,dlf->nlcd", pre_grad, up_local, preferred_element_type=jnp.float32
    )
    units = up_local.shape[1] * up_local.shape[2]
    return (
        up_grad.reshape(hidden_width, units),
        down_grad.reshape(units, hidden_width),
        partial_grads.reshape(owners, local_count * slot_count, hidden_width),
    )


def direct_plan(rows, cotangent, up_proj, down_proj, mix_weight, task_counts, expert_order):
    owners = lax.axis_size("expert")
    row_total = rows.shape[0]
    hidden_width = rows.shape[1]
    units = up_proj.shape[1]
    local_units = min(units, FF)
    local_count = max(units // FF, 1)
    copies = max(FF // units, 1)
    selection_index, slot_weight = block_route(
        task_counts[0], expert_order[0], mix_weight.reshape(-1), row_total
    )
    select_half = selection_index.astype(jnp.bfloat16)
    slot_row_values = jnp.dot(select_half, rows, preferred_element_type=jnp.float32).astype(
        jnp.bfloat16
    )
    slot_gradient_rows = jnp.dot(select_half, cotangent, preferred_element_type=jnp.float32)
    scaled = (slot_weight[:, None] * slot_gradient_rows).astype(jnp.bfloat16)
    upper_bound = lax.Precision.HIGHEST
    sent_rows = to_owners(slot_row_values.reshape(EXPERTS, CAP, hidden_width), copies, owners)
    sent_grads = to_owners(scaled.reshape(EXPERTS, CAP, hidden_width), copies, owners)
    up_local = up_proj.reshape(hidden_width, local_count, local_units)
    down_local = down_proj.reshape(local_count, local_units, hidden_width)
    got_rows = lax.all_to_all(sent_rows, "expert", split_axis=0, concat_axis=0, tiled=True)
    inputs, pre, act, outputs = forward_part(
        got_rows, up_local, down_local, owners, local_count, CAP
    )
    back_out = lax.all_to_all(outputs, "expert", split_axis=0, concat_axis=0, tiled=True)
    got_grads = lax.all_to_all(sent_grads, "expert", split_axis=0, concat_axis=0, tiled=True)
    up_full, down_full, partial_grads = backward_part(
        inputs, got_grads, pre, act, up_local, down_local, owners, local_count, CAP
    )
    back_grads = lax.all_to_all(partial_grads, "expert", split_axis=0, concat_axis=0, tiled=True)
    up_grad = up_full.astype(jnp.bfloat16)
    down_grad = down_full.astype(jnp.bfloat16)
    returned = from_owners(back_out, copies, hidden_width).reshape(EXPERTS * CAP, hidden_width)
    summed_grads = from_owners(back_grads, copies, hidden_width).reshape(
        EXPERTS * CAP, hidden_width
    )
    weighted_rows = returned * slot_weight[:, None]
    mixed = jnp.dot(selection_index.T, weighted_rows, precision=upper_bound).astype(jnp.bfloat16)
    row_gradient = jnp.dot(selection_index.T, summed_grads, precision=upper_bound).astype(
        jnp.bfloat16
    )
    return (mixed, row_gradient, up_grad, down_grad)


def grad_kernel(a_ref, b_ref, o_ref):
    o_ref[...] = lax.dot_general(
        a_ref[0], b_ref[0], (((0,), (0,)), ((), ())), preferred_element_type=jnp.float32
    ).astype(o_ref.dtype)


def cost(local_count, slots, units, width):
    return pl.CostEstimate(
        flops=2 * local_count * slots * units * width,
        bytes_accessed=2 * local_count * (units * width + slots * (units + width)),
        transcendentals=0,
    )


def up_grad_call(inputs, pre_grad):
    local_count, slots, width = inputs.shape
    units = pre_grad.shape[2]
    tile = min(512, units)
    return pl.pallas_call(
        grad_kernel,
        grid=(local_count, units // tile),
        in_specs=[
            pl.BlockSpec((1, slots, width), lambda l, j: (l, 0, 0)),
            pl.BlockSpec((1, slots, tile), lambda l, j: (l, 0, j)),
        ],
        out_specs=pl.BlockSpec((width, tile), lambda l, j: (0, l * (units // tile) + j)),
        out_shape=jax.ShapeDtypeStruct((width, local_count * units), jnp.bfloat16),
        cost_estimate=cost(local_count, slots, units, width),
    )(inputs, pre_grad)


def down_grad_call(act, scaled):
    local_count, slots, width = scaled.shape
    units = act.shape[2]
    tile = min(512, units)
    return pl.pallas_call(
        grad_kernel,
        grid=(local_count, units // tile),
        in_specs=[
            pl.BlockSpec((1, slots, tile), lambda l, j: (l, 0, j)),
            pl.BlockSpec((1, slots, width), lambda l, j: (l, 0, 0)),
        ],
        out_specs=pl.BlockSpec((tile, width), lambda l, j: (l * (units // tile) + j, 0)),
        out_shape=jax.ShapeDtypeStruct((local_count * units, width), jnp.bfloat16),
        cost_estimate=cost(local_count, slots, units, width),
    )(act, scaled)


def dot_nt(a, b):
    return lax.dot_general(a, b, (((1,), (1,)), ((), ())), preferred_element_type=jnp.float32)


def dot_tn(a, b):
    return lax.dot_general(a, b, (((0,), (0,)), ((), ())), preferred_element_type=jnp.float32)


def slot_places(counts, order, mix_flat, me, line, local_count, pad, row_total, width):
    task = jnp.arange(TASKS)
    firsts = jnp.sum(jnp.where(task[None, :] < task[:, None], counts[None, :], 0), axis=1)
    matches = order[None, :] == jnp.arange(EXPERTS, dtype=jnp.int32)[:, None]
    count_of = jnp.sum(jnp.where(matches, jnp.repeat(counts, K)[None], 0), axis=1)
    first_of = jnp.sum(jnp.where(matches, jnp.repeat(firsts, K)[None], 0), axis=1)
    weight_of = jnp.sum(jnp.where(matches, mix_flat[None], 0.0), axis=1)
    lane = jnp.arange(width, dtype=jnp.int32)
    member, local, spot = lane // pad % PLANE, lane // pad // PLANE, lane % pad
    slot = spot - (me // PLANE) * CAP
    known = (local < local_count) & (slot >= 0) & (slot < CAP)
    expert = (jnp.arange(line)[:, None] * PLANE + member[None]) * local_count + local[None]
    here = expert[:, :, None] == jnp.arange(EXPERTS, dtype=jnp.int32)
    spread = lambda v: jnp.sum(jnp.where(here, v[None, None], 0), axis=-1)
    filled = known[None] & (slot[None] < spread(count_of))
    target = jnp.where(filled, spread(first_of) + slot[None], -1).astype(jnp.float32)
    weight = jnp.where(filled, spread(weight_of), 0.0)
    high = lax.reduce_precision(weight, 8, 7)
    middle = lax.reduce_precision(weight - high, 8, 7)
    low = weight - high - middle
    return jnp.concatenate([target, high, middle, low]).astype(jnp.bfloat16)


def plane_kernel(
    line, local_count, pad,
    rows_ref, places_ref, cot_ref, up_hbm, down_hbm,
    mixed_ref, part_ref, x_out, s_out, act_out, pg_out,
    rows_all, cot_all, up_ref, down_ref, sel, w_ref, x_ref, s_ref, act_ref, pg_ref,
    x_send, s_send, o_send, d_send, o_got, d_got, pre_ref, acc_ref, m_send, m_got,
    w_sem, l_sem, out_sem, r_ss, r_rs, c_ss, c_rs, x_ss, x_rs, s_ss, s_rs, o_ss, o_rs, d_ss, d_rs, m_ss, m_rs,
):
    me = lax.axis_index("expert")
    z, p = me // PLANE, lax.rem(me, PLANE)
    row_total, width = cot_ref.shape
    f32, bf16 = jnp.float32, jnp.bfloat16

    weights_in = [
        pltpu.make_async_copy(up_hbm, up_ref, w_sem.at[0]),
        pltpu.make_async_copy(down_hbm, down_ref, w_sem.at[1]),
    ]
    own = [
        pltpu.make_async_copy(rows_ref, rows_all.at[z, pl.ds(0, row_total)], l_sem.at[0]),
        pltpu.make_async_copy(cot_ref, cot_all.at[z], l_sem.at[1]),
        pltpu.make_async_copy(
            places_ref, rows_all.at[z, pl.ds(row_total, places_ref.shape[0])], l_sem.at[2]
        ),
    ]
    for copy in own:
        copy.start()
    barrier = pltpu.get_barrier_semaphore()
    for k in range(1, PLANE):
        pl.semaphore_signal(barrier, inc=1, device_id={"expert": z * PLANE + lax.rem(p + k, PLANE)})
    for k in range(1, line):
        pl.semaphore_signal(barrier, inc=1, device_id={"expert": lax.rem(z + k, line) * PLANE + p})
    pl.semaphore_wait(barrier, PLANE - 1 + line - 1)
    for copy in own:
        copy.wait()
    for copy in weights_in:
        copy.start()

    def hop(buf, j, shift, ss, rs, lane):
        return pltpu.make_async_remote_copy(
            src_ref=buf.at[j], dst_ref=buf.at[j],
            send_sem=ss.at[lane, j], recv_sem=rs.at[j],
            device_id={"expert": lax.rem(me + (line + shift) * PLANE, line * PLANE)},
        )

    def pass_on(buf, j, shift, ss, rs):
        @pl.when((z + shift >= 0) & (z + shift < line))
        def _():
            hop(buf, j, shift, ss, rs, 0 if shift == 1 else 1).start()

    def settle(buf, ss, rs):
        for d in range(line):
            for shift in (1, -1):
                j = z - shift * d
                @pl.when((j >= 0) & (j < line) & (z + shift >= 0) & (z + shift < line))
                def _():
                    hop(buf, j, shift, ss, rs, 0 if shift == 1 else 1).wait_send()

    def gather_step(buf, d, ss, rs, after=None):
        for shift in (1, -1):
            j = z - shift * d
            @pl.when((j >= 0) & (j < line))
            def _():
                if d > 0:
                    hop(buf, j, shift, ss, rs, 0).wait_recv()
                pass_on(buf, j, shift, ss, rs)
            if after is not None:
                @pl.when(j == (0 if shift == 1 else line - 1))
                def _():
                    pass_on(after[0], z, shift, after[1], after[2])

    for d in range(line):
        gather_step(rows_all, d, r_ss, r_rs, (cot_all, c_ss, c_rs))

    lanes = sel.shape[1]
    weight = jnp.zeros((1, lanes), f32)
    for j in range(line):
        info = rows_all[j, row_total:, :lanes].astype(f32)
        at = lax.broadcasted_iota(jnp.int32, info.shape, 0)
        pick = lambda q: jnp.sum(jnp.where(at == q * line + z, info, 0.0), axis=0, keepdims=True)
        hit = lax.broadcasted_iota(jnp.int32, (row_total, lanes), 0) == pick(0).astype(jnp.int32)
        sel[j * row_total : (j + 1) * row_total, :] = jnp.where(hit, 1.0, 0.0).astype(bf16)
        weight += pick(1) + pick(2) + pick(3)
    w_ref[...] = jnp.transpose(jnp.broadcast_to(weight, (w_ref.shape[1], lanes)))

    def swap(send, got, ss, rs, l, k):
        to = lax.rem(p + k, PLANE)
        return pltpu.make_async_remote_copy(
            src_ref=send.at[l, pl.ds(pl.multiple_of(to * pad, 16), pad)],
            dst_ref=got.at[l, pl.ds(pl.multiple_of(p * pad, 16), pad)],
            send_sem=ss.at[l, k], recv_sem=rs.at[l, k],
            device_id={"expert": z * PLANE + to},
        )

    def keep(send, got, rs, l):
        place = pl.ds(pl.multiple_of(p * pad, 16), pad)
        return pltpu.make_async_copy(send.at[l, place], got.at[l, place], rs.at[l, 0])

    def swap_start(send, got, ss, rs, l):
        for k in range(1, PLANE):
            swap(send, got, ss, rs, l, k).start()
        keep(send, got, rs, l).start()

    def swap_wait(send, got, ss, rs, l):
        for k in range(1, PLANE):
            swap(send, got, ss, rs, l, k).wait()
        keep(send, got, rs, l).wait()

    taken = PLANE * pad

    def leave(ref, out, n, l):
        return pltpu.make_async_copy(ref.at[l], out.at[l], out_sem.at[n, l])

    def dispatch(values, scale, send, got, ss, rs):
        picked = dot_tn(sel[...], values)
        if scale is not None:
            picked = scale * picked
        picked = picked.astype(bf16)
        for l in range(local_count):
            send[l] = picked[l * taken : (l + 1) * taken]
        for l in range(local_count):
            swap_start(send, got, ss, rs, l)

    def forward(l):
        swap_wait(x_send, x_ref, x_ss, x_rs, l)
        leave(x_ref, x_out, 0, l).start()
        acc_ref[...] = jnp.zeros_like(acc_ref)

        @pl.loop(0, FF // TILE)
        def _(f):
            own_units = pl.ds(pl.multiple_of(f * TILE, TILE), TILE)
            units = pl.ds(pl.multiple_of(l * FF + f * TILE, TILE), TILE)
            pre = jnp.dot(x_ref[l], up_ref[:, units], preferred_element_type=f32)
            act = (pre / (1.0 + jnp.exp(-pre))).astype(bf16)
            pre_ref[l, :, own_units] = pre
            act_ref[l, :, own_units] = act
            acc_ref[...] += jnp.dot(act, down_ref[units, :], preferred_element_type=f32)

        o_send[l] = acc_ref[...].astype(bf16)
        swap_start(o_send, o_got, o_ss, o_rs, l)
        leave(act_ref, act_out, 2, l).start()

    dispatch(
        rows_all[:, :row_total, :].reshape(line * row_total, width), None, x_send, x_ref, x_ss, x_rs
    )
    for d in range(1, line - 1):
        gather_step(cot_all, d, c_ss, c_rs)
    for copy in weights_in:
        copy.wait()
    forward(0)
    gather_step(cot_all, line - 1, c_ss, c_rs)
    dispatch(
        cot_all[...].reshape(line * row_total, width), w_ref[:, :1], s_send, s_ref, s_ss, s_rs
    )
    for l in range(1, local_count):
        forward(l)

    def back(l):
        swap_wait(s_send, s_ref, s_ss, s_rs, l)
        leave(s_ref, s_out, 1, l).start()
        acc_ref[...] = jnp.zeros_like(acc_ref)

        @pl.loop(0, FF // TILE)
        def _(f):
            own_units = pl.ds(pl.multiple_of(f * TILE, TILE), TILE)
            units = pl.ds(pl.multiple_of(l * FF + f * TILE, TILE), TILE)
            act_grad = dot_nt(s_ref[l], down_ref[units, :])
            pre = pre_ref[l, :, own_units]
            sg = 1.0 / (1.0 + jnp.exp(-pre))
            pre_grad = (act_grad * sg * (1.0 + pre * (1.0 - sg))).astype(bf16)
            pg_ref[l, :, own_units] = pre_grad
            acc_ref[...] += dot_nt(pre_grad, up_ref[:, units])

        d_send[l] = acc_ref[...].astype(bf16)
        swap_start(d_send, d_got, d_ss, d_rs, l)
        leave(pg_ref, pg_out, 3, l).start()

    def combined(slots):
        total = jnp.dot(sel[...], slots, preferred_element_type=f32)
        return total.astype(bf16).reshape(line, row_total, width)

    def home(k):
        to = lax.rem(z + k, line)
        return pltpu.make_async_remote_copy(
            src_ref=m_send.at[to], dst_ref=m_got.at[z],
            send_sem=m_ss.at[k], recv_sem=m_rs.at[k],
            device_id={"expert": to * PLANE + p},
        )

    back(0)
    for l in range(local_count):
        swap_wait(o_send, o_got, o_ss, o_rs, l)
    outs = o_got[...].reshape(lanes, width).astype(f32)
    m_send[...] = combined((w_ref[:, :1] * outs).astype(bf16))
    for k in range(1, line):
        home(k).start()
    keep_mixed = pltpu.make_async_copy(m_send.at[z], m_got.at[z], m_rs.at[0])
    keep_mixed.start()
    for l in range(1, local_count):
        back(l)
    for l in range(local_count):
        swap_wait(d_send, d_got, d_ss, d_rs, l)
    part_ref[...] = combined(d_got[...].reshape(lanes, width))
    for k in range(1, line):
        home(k).wait()
    keep_mixed.wait()
    mixed_ref[...] = sum(m_got[j].astype(f32) for j in range(line)).astype(bf16)
    settle(rows_all, r_ss, r_rs)
    settle(cot_all, c_ss, c_rs)
    for l in range(local_count):
        for n, (ref, out) in enumerate(
            ((x_ref, x_out), (s_ref, s_out), (act_ref, act_out), (pg_ref, pg_out))
        ):
            leave(ref, out, n, l).wait()


def plane_call(rows, places, cotangent, up_proj, down_proj, line, local_count, pad):
    bf16, f32 = jnp.bfloat16, jnp.float32
    row_total, width = cotangent.shape
    taken = PLANE * pad
    slots = (local_count, taken, width)
    wide = (local_count, taken, FF)
    dma = pltpu.SemaphoreType.DMA
    vmem, anywhere = pl.BlockSpec(memory_space=pltpu.VMEM), pl.BlockSpec(memory_space=pl.ANY)
    lanes = local_count * taken
    blocks = (line, row_total, width)
    swaps = (local_count, PLANE)
    return pl.pallas_call(
        functools.partial(plane_kernel, line, local_count, pad),
        out_shape=[
            jax.ShapeDtypeStruct((row_total, width), bf16),
            jax.ShapeDtypeStruct(blocks, bf16),
            jax.ShapeDtypeStruct(slots, bf16),
            jax.ShapeDtypeStruct(slots, bf16),
            jax.ShapeDtypeStruct(wide, bf16),
            jax.ShapeDtypeStruct(wide, bf16),
        ],
        in_specs=[vmem, vmem, vmem, anywhere, anywhere],
        out_specs=[vmem] * 2 + [anywhere] * 4,
        scratch_shapes=[
            pltpu.VMEM((line, row_total + places.shape[0], width), bf16),
            pltpu.VMEM(blocks, bf16),
            pltpu.VMEM(up_proj.shape, bf16),
            pltpu.VMEM(down_proj.shape, bf16),
        ]
        + [pltpu.VMEM((line * row_total, lanes), bf16), pltpu.VMEM((lanes, 128), f32)]
        + [pltpu.VMEM(slots, bf16)] * 2
        + [pltpu.VMEM(wide, bf16)] * 2
        + [pltpu.VMEM(slots, bf16)] * 6
        + [pltpu.VMEM(wide, f32), pltpu.VMEM((taken, width), f32)]
        + [pltpu.VMEM(blocks, bf16)] * 2
        + [dma((2,)), dma((3,)), dma((4, local_count))]
        + [dma((2, line)), dma((line,))] * 2
        + [dma(swaps)] * 8
        + [dma((line,))] * 2,
        compiler_params=pltpu.CompilerParams(
            collective_id=0, has_side_effects=True, vmem_limit_bytes=60 << 20
        ),
    )(rows, places, cotangent, up_proj, down_proj)


def plane_plan(rows, cotangent, up_proj, down_proj, mix_weight, task_counts, expert_order):
    owners = lax.axis_size("expert")
    me = lax.axis_index("expert")
    line = owners // PLANE
    row_total, width = rows.shape
    local_count = up_proj.shape[1] // FF
    pad = (line * CAP + 15) // 16 * 16
    places = slot_places(
        task_counts[0], expert_order[0], mix_weight.reshape(-1),
        me, line, local_count, pad, row_total, width,
    )
    mixed, parts, inputs, scaled, act, pre_grad = plane_call(
        rows, places, cotangent, up_proj, down_proj, line, local_count, pad
    )
    groups = [[z * PLANE + p for z in range(line)] for p in range(PLANE)]
    home = lax.all_to_all(parts, "expert", 0, 0, axis_index_groups=groups, tiled=True)
    up_grad = up_grad_call(inputs, pre_grad)
    down_grad = down_grad_call(act, scaled)
    row_gradient = jnp.sum(home.astype(jnp.float32), axis=0).astype(jnp.bfloat16)
    return (mixed, row_gradient, up_grad, down_grad)


def per_device(rows, cotangent, up_proj, *others):
    owners = lax.axis_size("expert")
    whole_experts = up_proj.shape[1] % FF == 0
    local_count = up_proj.shape[1] // FF
    fits = owners % PLANE == 0 and local_count * -(-owners // PLANE * CAP // 16) * 16 * PLANE <= rows.shape[1]
    wide_plane = fits and owners > PLANE
    plan = plane_plan if whole_experts and wide_plane else direct_plan
    return plan(rows, cotangent, up_proj, *others)


def solution(mesh):
    return jax.shard_map(
        per_device,
        mesh=mesh,
        in_specs=(
            P(("group", "expert"), None),
            P(("group", "expert"), None),
            P(None, "expert"),
            P("expert", None),
            P(),
            P(("group", "expert"), None),
            P(("group", "expert"), None),
        ),
        out_specs=(
            P(("group", "expert"), None),
            P(("group", "expert"), None),
            P("group", "expert"),
            P("expert", "group"),
        ),
        check_vma=False,
    )
```
